32 devices in a mesh: win: 2 (over y), row: 16 (over z, x, core).
Axes of the slice: x: 2, y: 2, z: 4, core: 2. Of those that a mesh axis runs over, the one named last changes fastest.
Arguments:
- image: float32 [3, 2048, 4096], P(None, ('win', 'row')), parts along dimension 1, may hold values from -6 to 6
- grad_x: bfloat16 [3, 2048, 4096], P(None, ('win', 'row')), parts along dimension 1, may hold values from -6 to 6
- grad_y: bfloat16 [3, 2048, 4096], P(None, ('win', 'row')), parts along dimension 1, may hold values from -6 to 6
- classes: int32 [2048, 4096], P(('win', 'row')), parts along dimension 0, may hold values from 0 to 3
- validity: int32 [2, 4], P('win'), parts along dimension 0, may hold values 0 or 1
- owners: int32 [2, 4, 2], P('win'), parts along dimension 0, may hold values from 0 to 1
Outputs:
- solution: float32 [3, 2048, 4096], P(None, ('win', 'row')), parts along dimension 1
The draws below stay inside these ranges and needn't reach their ends.
There are 2 independent parts, one for each index of `win`. The reference program is written for one: setup_inputs(seed, part) draws one part's arguments, and reference() takes and returns one part's arrays. A program takes and returns all parts, laid end to end along the dimension named above; each array names one. Nothing has to cross between parts.
All inputs are finite; a program needn't handle non-finite values.
Results may differ from the reference program's by a relative error of at most 0.0003.
Values may be sent and summed in bfloat16 or wider, within the bound.
No kernel may reach another device: no remote copies, remote signals or barrier semaphores. Data moves between devices by JAX's collectives and lax.ppermute only.
A program may use at most 128 MiB of HBM per device.

```python
import jax
import jax.numpy as jnp

TILE_ROWS = 1024
TILE_COLS = 1024
TILES_X = 4
BAND = 48
SWEEPS = 4
HEIGHT = 1024
WIDTH = 4096
TILES_Y = 1


def set_ends(drawn, key, least, largest):
    dims = drawn.shape
    place = [jax.random.randint(jax.random.fold_in(key, axis), (), 0, dims[axis]) for axis in range(len(dims))]
    drawn = drawn.at[tuple(place)].set(least)
    longest = dims.index(max(dims))
    place[longest] = (place[longest] + 1) % dims[longest]
    return drawn.at[tuple(place)].set(largest)


def levels(own_key, dims, split, least, top_value):
    def one(position, blocks):
        heights = jax.random.uniform(jax.random.fold_in(jax.random.fold_in(own_key, 6), position), (blocks,), jnp.float32, least / len(split), top_value / len(split))
        return jnp.repeat(jnp.exp(heights), dims[position] // blocks).reshape((-1,) + (1,) * (len(dims) - position - 1))

    level = one(*split[0])
    for cut in split[1:]:
        level = level * one(*cut)
    return level


def gaussian(rng, dims, width, most, pieces=(), dtype=jnp.bfloat16):
    loudness = levels(rng, dims, pieces, -0.22, 0.18) if pieces else 1.0
    drawn = jax.random.normal(rng, dims, jnp.float32) * width * loudness
    return jnp.minimum(jnp.maximum(drawn, -most), most).astype(dtype)


def setup_inputs(seed: int = 0, part: int = 0) -> dict:
    key_list = jax.random.split(jax.random.key(seed), 7)
    own_keys = jax.random.split(jax.random.fold_in(key_list[6], part), 7)
    image = gaussian(own_keys[0], (3, HEIGHT, WIDTH), 1.0, 6.0, ((1, 16),), jnp.float32)
    grad_x = gaussian(own_keys[1], (3, HEIGHT, WIDTH), 1.0, 6.0, ((1, 16),))
    grad_y = gaussian(own_keys[2], (3, HEIGHT, WIDTH), 1.0, 6.0, ((1, 16),))
    classes = set_ends(jax.random.randint(own_keys[3], (HEIGHT, WIDTH), 0, 4), jax.random.fold_in(own_keys[3], 1), 0, 3).astype(jnp.int32)
    validity = set_ends((jax.random.randint(own_keys[4], (TILES_Y, TILES_X), 0, 4) < 3).astype(jnp.int32), jax.random.fold_in(own_keys[4], 1), 0, 1)
    owners = set_ends(jax.random.randint(own_keys[5], (TILES_Y, TILES_X, 2), 0, 2), jax.random.fold_in(own_keys[5], 1), 0, 1).astype(jnp.int32)
    return dict(image=image, grad_x=grad_x, grad_y=grad_y, classes=classes, validity=validity, owners=owners)


OMEGA = 0.8
SCREEN = 0.25


def blend_seams(horizontal, vertical, owners):
    vert_tiles = vertical.reshape(3, TILES_Y, TILE_ROWS, WIDTH)
    upper_mean = jnp.mean(vert_tiles[:, :-1, TILE_ROWS - 1 - BAND:TILE_ROWS - 1, :], axis=2)
    lower_mean = jnp.mean(vert_tiles[:, 1:, :BAND, :], axis=2)
    lower_owns = jnp.repeat(owners[:-1, :, 0], TILE_COLS, axis=1)[None] == 1
    vert_tiles = vert_tiles.at[:, :-1, TILE_ROWS - 1, :].set(jnp.where(lower_owns, lower_mean, upper_mean))
    horiz_tiles = horizontal.reshape(3, HEIGHT, TILES_X, TILE_COLS)
    left_mean = jnp.mean(horiz_tiles[:, :, :-1, TILE_COLS - 1 - BAND:TILE_COLS - 1], axis=3)
    right_mean = jnp.mean(horiz_tiles[:, :, 1:, :BAND], axis=3)
    right_owns = jnp.repeat(owners[:, :-1, 1], TILE_ROWS, axis=0)[None] == 1
    horiz_tiles = horiz_tiles.at[:, :, :-1, TILE_COLS - 1].set(jnp.where(right_owns, right_mean, left_mean))
    return horiz_tiles.reshape(3, HEIGHT, WIDTH), vert_tiles.reshape(3, HEIGHT, WIDTH)


def divergence(horiz_pad, vert_pad):
    horiz_here = horiz_pad[:, 1:, 1:-1]
    horiz_left = horiz_pad[:, 1:, :-2]
    horiz_above = horiz_pad[:, :-1, 1:-1]
    horiz_corner = horiz_pad[:, :-1, :-2]
    vert_here = vert_pad[:, 1:, 1:-1]
    vert_right = vert_pad[:, 1:, 2:]
    vert_left = vert_pad[:, 1:, :-2]
    vert_above = vert_pad[:, :-1, 1:-1]
    diagonal = horiz_here + vert_right - horiz_corner - vert_above + vert_left - horiz_left - vert_above + horiz_above
    return horiz_here - horiz_left + vert_here - vert_above + 0.5 * diagonal


def neighbours(padded):
    axial = padded[:, :-2, 1:-1] + padded[:, 2:, 1:-1] + padded[:, 1:-1, :-2] + padded[:, 1:-1, 2:]
    corner = padded[:, :-2, :-2] + padded[:, :-2, 2:] + padded[:, 2:, :-2] + padded[:, 2:, 2:]
    return axial + 0.5 * corner


def relax(row_padded, target, div_term, weights):
    current = row_padded[:, 1:-1, :]
    padded = jnp.pad(row_padded, ((0, 0), (0, 0), (1, 1)))
    return (1.0 - OMEGA) * current + OMEGA * (weights * target + neighbours(padded) - div_term) / (weights + 6.0)


def reference(image, grad_x, grad_y, classes, validity, owners):
    horizontal, vertical = blend_seams(grad_x.astype(jnp.float32), grad_y.astype(jnp.float32), owners)
    mean_vert = jnp.mean(vertical, axis=2)
    mean_image = jnp.mean(image, axis=2)
    level = jnp.cumsum(mean_vert, axis=1) - mean_vert - mean_image + mean_image[:, :1]
    target = image + level[:, :, None]
    cover = jnp.repeat(jnp.repeat(validity, TILE_ROWS, axis=0), TILE_COLS, axis=1).astype(jnp.float32)
    weights = cover * SCREEN * jnp.exp2(classes.astype(jnp.float32))
    edge = ((0, 0), (1, 0), (1, 1))
    div_term = divergence(jnp.pad(horizontal, edge), jnp.pad(vertical, edge))
    solution = target
    for sweep in range(SWEEPS):
        solution = relax(jnp.pad(solution, ((0, 0), (1, 1), (0, 0))), target, div_term, weights)
    return solution
```

```python
import jax
import jax.numpy as jnp
from jax import lax
from jax.experimental import pallas as pl
from jax.experimental.pallas import tpu as pltpu
from jax.sharding import PartitionSpec as P

TILE_ROWS = 1024
TILE_COLS = 1024
BAND = 48
SWEEPS = 4
OMEGA = 0.8
SCREEN = 0.25

LANES = 128
HALO = SWEEPS
TOP = 8
FIRST = TOP + HALO
f32 = jnp.float32
bf16 = jnp.bfloat16


def lane_tile(j):
    return slice(j * LANES, (j + 1) * LANES)


def sublane_ids():
    return lax.broadcasted_iota(jnp.int32, (8, LANES), 0)


def lane_ids():
    return lax.broadcasted_iota(jnp.int32, (8, LANES), 1)


def pack_kernel(image, gx, gy, classes, gy_all, to_a, to_b, sums, img_e, gx_e, gy_e, cls_e, sem):
    channels, rows, width = image.shape
    tiles = width // LANES
    position = lax.axis_index("row")
    even = position % 2 == 0
    copies = []
    for side, start in enumerate((0, rows - 8)):
        window = pl.ds(start, 8)
        for n, (src, dst) in enumerate(((image, img_e), (gx, gx_e), (gy, gy_e))):
            copies.append(pltpu.make_async_copy(src.at[:, window, :], dst.at[side], sem.at[side, n]))
        copies.append(pltpu.make_async_copy(classes.at[window, :], cls_e.at[side], sem.at[side, 3]))
    for copy in copies:
        copy.start()
    low_half = sublane_ids() < 4
    for k in range(channels):
        total = jnp.zeros((8, LANES), f32)

        def add_rows(g, acc):
            for j in range(tiles):
                x = gy_all[k, pl.ds(g * 16, 16), lane_tile(j)].astype(f32)
                acc = acc + (x[:8] + x[8:])
            return acc

        total = lax.fori_loop(0, rows // 16, add_rows, total)
        total = jnp.sum(jnp.sum(total, axis=1, keepdims=True), axis=0, keepdims=True) / width
        sums[k : k + 1, :] = jnp.broadcast_to(total, (1, LANES))
    for copy in copies:
        copy.wait()
    for k in range(channels):
        lead = jnp.zeros((8, LANES), f32)
        for j in range(tiles):
            lead = lead + img_e[0, k, :, lane_tile(j)]
        lead = jnp.sum(lead[0:1, :], axis=1, keepdims=True) / width
        lead = jnp.where(position == 0, lead, 0.0)
        sums[channels + k : channels + k + 1, :] = jnp.broadcast_to(lead, (1, LANES))
    if 2 * channels < 8:
        sums[2 * channels :, :] = jnp.zeros((8 - 2 * channels, LANES), f32)

    def joined(side, first, second):
        if side == 0:
            return jnp.where(low_half, first, pltpu.roll(second, 4, 0))
        return jnp.where(low_half, pltpu.roll(first, 4, 0), second)

    def fill(side, out):
        def one(j):
            at = pl.ds(pl.multiple_of(j * LANES, LANES), LANES)
            for k in range(channels):
                x = img_e[side, k, :, at]
                high = x.astype(bf16).astype(f32)
                out[2 * k, :, at] = joined(side, high, x - high).astype(bf16)
                out[2 * k + 1, :, at] = joined(
                    side, gx_e[side, k, :, at].astype(f32), gy_e[side, k, :, at].astype(f32)
                ).astype(bf16)
            c = cls_e[side, :, at].astype(f32)
            out[2 * channels, :, at] = joined(side, c, c).astype(bf16)

        def step(j, carry):
            one(j)
            return carry

        lax.fori_loop(0, tiles, step, 0, unroll=4)

    @pl.when(even)
    def _():
        fill(1, to_a)
        fill(0, to_b)

    @pl.when(jnp.logical_not(even))
    def _():
        fill(0, to_a)
        fill(1, to_b)


def pack(image, gx, gy, classes):
    channels, rows, width = image.shape
    hbm = pl.BlockSpec(memory_space=pl.ANY)
    edge = jax.ShapeDtypeStruct((2 * channels + 1, 8, width), bf16)
    return pl.pallas_call(
        pack_kernel,
        out_shape=(edge, edge, jax.ShapeDtypeStruct((8, LANES), f32)),
        in_specs=[hbm, hbm, hbm, hbm, pl.BlockSpec(memory_space=pltpu.VMEM)],
        out_specs=[pl.BlockSpec(memory_space=pltpu.VMEM)] * 3,
        scratch_shapes=[
            pltpu.VMEM((2, channels, 8, width), f32),
            pltpu.VMEM((2, channels, 8, width), bf16),
            pltpu.VMEM((2, channels, 8, width), bf16),
            pltpu.VMEM((2, 8, width), jnp.int32),
            pltpu.SemaphoreType.DMA((2, 4)),
        ],
        name="pack",
    )(image, gx, gy, classes, gy)


def main_kernel(
    validity, owners, offset, from_a, from_b, image, gx, gy, classes, out,
    halo, q_s, qw_s, x_s, y_s, s_s, t_s, b_s, row_y, row_i, level, sem,
):
    channels = pl.num_programs(0)
    k = pl.program_id(0)
    _, rows, width = image.shape
    tiles = width // LANES
    per_tile = TILE_COLS // LANES
    groups = (rows + 2 * HALO) // 8
    n_classes = 6
    position = lax.axis_index("row")
    last = lax.axis_size("row") - 1
    even = position % 2 == 0
    above = position > 0
    below = position < last
    tile_row = position * rows // TILE_ROWS
    lanes = lane_ids()
    first_lane = lanes == 0
    last_lane = lanes == LANES - 1

    @pl.when(k == 0)
    def _():
        @pl.when(even)
        def _():
            pltpu.make_async_copy(from_b, halo.at[0], sem.at[0]).start()
            pltpu.make_async_copy(from_a, halo.at[1], sem.at[1]).start()

        @pl.when(jnp.logical_not(even))
        def _():
            pltpu.make_async_copy(from_a, halo.at[0], sem.at[0]).start()
            pltpu.make_async_copy(from_b, halo.at[1], sem.at[1]).start()

        for ref in (q_s, qw_s, x_s, y_s, s_s, t_s, b_s):
            for j in range(tiles):
                ref[j, 0:8, :] = jnp.zeros((8, LANES), f32)
                ref[j, TOP + 8 * groups : TOP + 8 * groups + 8, :] = jnp.zeros((8, LANES), f32)

    def factors(c, cover):
        w = cover * SCREEN * jnp.exp2(c)
        q = OMEGA / (w + 6.0)
        return q, q * w

    @pl.when(k == 0)
    def _():
        covers = [validity[tile_row, b].astype(f32) for b in range(width // TILE_COLS)]

        def natural(g, carry):
            at = pl.multiple_of(g * 8, 8)
            for j in range(tiles):
                q, qw = factors(classes[pl.ds(at, 8), lane_tile(j)].astype(f32), covers[j // per_tile])
                q_s[j, pl.ds(FIRST + at, 8), :] = q
                qw_s[j, pl.ds(FIRST + at, 8), :] = qw
            return carry

        lax.fori_loop(0, rows // 8, natural, 0)
        pltpu.make_async_copy(from_a, halo.at[0], sem.at[0]).wait()
        pltpu.make_async_copy(from_a, halo.at[1], sem.at[1]).wait()
        for side, there, at in ((0, above, TOP), (1, below, FIRST + rows)):
            beyond = jnp.where(
                side == 0,
                jnp.maximum(position * rows - 1, 0) // TILE_ROWS,
                jnp.minimum((position + 1) * rows, (last + 1) * rows - 1) // TILE_ROWS,
            )
            for j in range(tiles):
                cover = validity[beyond, j // per_tile].astype(f32)
                q, qw = factors(halo[side, n_classes, :, lane_tile(j)].astype(f32), cover)
                q_s[j, at : at + HALO, :] = jnp.where(there, q, 0.0)[:HALO]
                qw_s[j, at : at + HALO, :] = jnp.where(there, qw, 0.0)[:HALO]

    def unpack(g, carry):
        at = pl.multiple_of(g * 16, 16)
        sum_y = jnp.zeros((16, LANES), f32)
        sum_i = jnp.zeros((16, LANES), f32)
        for j in range(tiles):
            here = pl.ds(FIRST + at, 16)
            x_s[j, here, :] = gx[0, pl.ds(at, 16), lane_tile(j)].astype(f32)
            y = gy[0, pl.ds(at, 16), lane_tile(j)].astype(f32)
            y_s[j, here, :] = y
            i = image[0, pl.ds(at, 16), lane_tile(j)]
            s_s[j, here, :] = i
            sum_y = sum_y + y
            sum_i = sum_i + i
        row_y[pl.ds(FIRST + at, 16), :] = sum_y
        row_i[pl.ds(FIRST + at, 16), :] = sum_i
        return carry

    lax.fori_loop(0, rows // 16, unpack, 0)
    for side, at in ((0, TOP), (1, FIRST + rows)):
        sum_y = jnp.zeros((8, LANES), f32)
        sum_i = jnp.zeros((8, LANES), f32)
        for j in range(tiles):
            v = halo[side, 2 * k, :, lane_tile(j)].astype(f32)
            i = v + pltpu.roll(v, 4, 0)
            s_s[j, at : at + HALO, :] = i[:HALO]
            g = halo[side, 2 * k + 1, :, lane_tile(j)].astype(f32)
            y = pltpu.roll(g, 4, 0)
            x_s[j, at : at + HALO, :] = g[:HALO]
            y_s[j, at : at + HALO, :] = y[:HALO]
            sum_y = sum_y + y
            sum_i = sum_i + i
        row_y[at : at + HALO, :] = sum_y[:HALO]
        row_i[at : at + HALO, :] = sum_i[:HALO]

    for b in range(width // TILE_COLS - 1):
        j = (b + 1) * per_tile - 1
        for g in range(groups):
            at = TOP + 8 * g
            if g == 0:
                other = jnp.maximum(position * rows - 1, 0) // TILE_ROWS
            elif g == groups - 1:
                other = jnp.minimum((position + 1) * rows, (last + 1) * rows - 1) // TILE_ROWS
            else:
                other = tile_row
            left = x_s[j, at : at + 8, :]
            right = x_s[j + 1, at : at + 8, :]
            right_sum = jnp.sum(jnp.where(lanes < BAND, right, 0.0), axis=1, keepdims=True)
            left_sum = jnp.sum(
                jnp.where((lanes >= LANES - 1 - BAND) & (lanes < LANES - 1), left, 0.0), axis=1, keepdims=True
            )
            own = jnp.where(owners[tile_row, b, 1] == 1, right_sum, left_sum)
            if g in (0, groups - 1):
                far = jnp.where(owners[other, b, 1] == 1, right_sum, left_sum)
                half = sublane_ids() < HALO
                own = jnp.where(half == (g == 0), far, own)
            x_s[j, at : at + 8, :] = jnp.where(last_lane, own / BAND, left)

    r = lax.broadcasted_iota(jnp.int32, (8 * groups, 8 * groups), 0)
    c = lax.broadcasted_iota(jnp.int32, (8 * groups, 8 * groups), 1)
    reach = jnp.where((c < r) & (c >= HALO), 1.0, jnp.where((c >= r) & (c < HALO), -1.0, 0.0))
    span = slice(TOP, TOP + 8 * groups)
    climbed = jnp.dot(reach, row_y[span, :], precision=lax.Precision.HIGHEST, preferred_element_type=f32)
    lv = jnp.sum(climbed - row_i[span, :], axis=1, keepdims=True) / width
    lv = jnp.broadcast_to(lv, (8 * groups, LANES)) + (
        offset[pl.ds(k, 1), :] + offset[pl.ds(k + channels, 1), :]
    )
    row = lax.broadcasted_iota(jnp.int32, (8 * groups, LANES), 0) - HALO
    inside = ((row >= 0) | above) & ((row < rows) | below)
    level[...] = jnp.where(inside, lv, 0.0)

    def shifted(prev, rots, nxt, j):
        pass

    def terms(g, carry):
        at = pl.multiple_of(TOP + g * 8, 8)
        lv = level[pl.ds(pl.multiple_of(g * 8, 8), 8), :]
        fs, ys = [], []
        left_t = right_y = None

        def load(j):
            x = x_s[j, pl.ds(at, 8), :]
            xu = x_s[j, pl.ds(at - 1, 8), :]
            y = y_s[j, pl.ds(at, 8), :]
            yu = y_s[j, pl.ds(at - 1, 8), :]
            f = 3.0 * x + xu
            base = f + 2.0 * (y - 2.0 * yu)
            return base, pltpu.roll(y - f, 1, 1), pltpu.roll(y, LANES - 1, 1)

        zero = jnp.zeros((8, LANES), f32)
        prev_rot = zero
        cur = load(0)
        for j in range(tiles):
            nxt = load(j + 1) if j + 1 < tiles else (None, None, zero)
            base, rot_l, rot_r = cur
            twice = base + jnp.where(first_lane, prev_rot, rot_l) + jnp.where(last_lane, nxt[2], rot_r)
            q = q_s[j, pl.ds(at, 8), :]
            qw = qw_s[j, pl.ds(at, 8), :]
            t = s_s[j, pl.ds(at, 8), :] + lv
            s_s[j, pl.ds(at, 8), :] = t
            b_s[j, pl.ds(at, 8), :] = qw * t - (0.5 * q) * twice
            prev_rot = rot_l
            cur = nxt
        return carry

    lax.fori_loop(0, groups, terms, 0)

    def sweep(src, write, count, start):
        def body(g, carry):
            at = start + g * 8

            def load(j):
                s = src[j, pl.ds(at, 8), :]
                u = src[j, pl.ds(at - 1, 8), :] + src[j, pl.ds(at + 1, 8), :]
                a = s + 0.5 * u
                return s, u, pltpu.roll(a, 1, 1), pltpu.roll(a, LANES - 1, 1)

            zero = jnp.zeros((8, LANES), f32)
            prev_rot = zero
            cur = load(0)
            for j in range(tiles):
                nxt = load(j + 1) if j + 1 < tiles else (None, None, None, zero)
                s, u, rot_l, rot_r = cur
                n = u + jnp.where(first_lane, prev_rot, rot_l) + jnp.where(last_lane, nxt[3], rot_r)
                new = (1.0 - OMEGA) * s + (q_s[j, pl.ds(at, 8), :] * n + b_s[j, pl.ds(at, 8), :])
                write(g, j, at, new)
                prev_rot = rot_l
                cur = nxt
            return carry

        lax.fori_loop(0, count, body, 0)

    def into(dst):
        def write(g, j, at, v):
            dst[j, pl.ds(at, 8), :] = v

        return write

    def finish(g, j, at, v):
        out[0, pl.ds(pl.multiple_of(g * 8, 8), 8), lane_tile(j)] = v

    src, dst = s_s, t_s
    for _ in range(SWEEPS - 1):
        sweep(src, into(dst), groups, TOP)
        src, dst = dst, src
    sweep(src, finish, rows // 8, FIRST)


def relax(validity, owners, offset, from_a, from_b, image, gx, gy, classes):
    channels, rows, width = image.shape
    tiles = width // LANES
    tall = TOP + rows + 2 * HALO + 8
    smem = pl.BlockSpec(memory_space=pltpu.SMEM)
    hbm = pl.BlockSpec(memory_space=pl.ANY)
    channel = pl.BlockSpec((1, rows, width), lambda k: (k, 0, 0))
    big = pltpu.VMEM((tiles, tall, LANES), f32)
    return pl.pallas_call(
        main_kernel,
        grid=(channels,),
        out_shape=jax.ShapeDtypeStruct(image.shape, f32),
        in_specs=[
            smem, smem, pl.BlockSpec(memory_space=pltpu.VMEM), hbm, hbm,
            channel, channel, channel, pl.BlockSpec((rows, width), lambda k: (0, 0)),
        ],
        out_specs=channel,
        scratch_shapes=[
            pltpu.VMEM((2,) + from_a.shape, bf16),
            big, big, big, big, big, big, big,
            pltpu.VMEM((tall, LANES), f32),
            pltpu.VMEM((tall, LANES), f32),
            pltpu.VMEM((rows + 2 * HALO, LANES), f32),
            pltpu.SemaphoreType.DMA((2,)),
        ],
        name="relax",
    )(validity, owners, offset, from_a, from_b, image, gx, gy, classes)


def pairs_with(offset, devices):
    pairs = []
    for i in range(offset, devices - 1, 2):
        pairs += [(i, i + 1), (i + 1, i)]
    return pairs


def carried_in(sums, channels):
    devices = lax.axis_size("row")
    position = lax.axis_index("row")
    is_total = lax.broadcasted_iota(jnp.int32, sums.shape, 0) < channels
    held, carried = sums, jnp.where(is_total, 0.0, sums)
    by = 1
    while by < devices:
        pairs = [(i, i ^ by) for i in range(devices) if (i ^ by) < devices]
        other = lax.ppermute(held, "row", pairs)
        lower = (position & by) != 0
        carried = carried + jnp.where(is_total & jnp.logical_not(lower), 0.0, other)
        held = held + other
        by *= 2
    return carried


def blended_last_row(gy, owners):
    rows, width = gy.shape[1:]
    devices, position = lax.axis_size("row"), lax.axis_index("row")
    vertical = gy.astype(f32)
    own = lax.dynamic_index_in_dim(owners, position * rows // TILE_ROWS, 0, keepdims=False)
    pairs = [(i, i - 1) for i in range(1, devices)]
    lower = lax.ppermute(jnp.mean(vertical[:, :BAND], axis=1).astype(bf16), "row", pairs)
    upper = jnp.mean(vertical[:, rows - 1 - BAND : rows - 1], axis=1).astype(bf16)
    lower_owns = jnp.repeat(own[:, 0], TILE_COLS, total_repeat_length=width)[None] == 1
    at_seam = (((position + 1) * rows) % TILE_ROWS == 0) & (position < devices - 1)
    last = jnp.where(at_seam, jnp.where(lower_owns, lower, upper), gy[:, -1])
    return gy.at[:, -1].set(last)


def per_device(image, grad_x, grad_y, classes, validity, owners):
    channels, rows, _ = image.shape
    devices = lax.axis_size("row")
    if devices * rows > TILE_ROWS:
        grad_y = blended_last_row(grad_y, owners)
    to_a, to_b, sums = pack(image, grad_x, grad_y, classes)
    from_a = lax.ppermute(to_a, "row", pairs_with(0, devices))
    from_b = lax.ppermute(to_b, "row", pairs_with(1, devices))
    offset = carried_in(sums, channels)
    return relax(validity, owners, offset, from_a, from_b, image, grad_x, grad_y, classes)


def solution(mesh):
    split = ("win", "row")
    in_specs = (
        P(None, split, None), P(None, split, None), P(None, split, None),
        P(split, None), P("win", None), P("win", None, None),
    )
    return jax.shard_map(
        per_device, mesh=mesh, in_specs=in_specs, out_specs=P(None, split, None), check_vma=False
    )
```

```python
import jax
import jax.numpy as jnp
from jax import lax
from jax.experimental import pallas as pl
from jax.experimental.pallas import tpu as pltpu
from jax.sharding import PartitionSpec as P

TILE_ROWS = 1024
TILE_COLS = 1024
BAND = 48
SWEEPS = 4
OMEGA = 0.8
SCREEN = 0.25

LANES = 128
HALO = SWEEPS
TOP = 8
FIRST = TOP + HALO
SCOPED = 16 << 20
f32 = jnp.float32
bf16 = jnp.bfloat16


def lane_tile(j):
    return slice(j * LANES, (j + 1) * LANES)


def sublane_ids():
    return lax.broadcasted_iota(jnp.int32, (8, LANES), 0)


def lane_ids():
    return lax.broadcasted_iota(jnp.int32, (8, LANES), 1)


def pack_kernel(image, gx, classes, gy, to_a, to_b, sums, img_e, gx_e, cls_e, sem):
    channels, rows, width = image.shape
    tiles = width // LANES
    position = lax.axis_index("row")
    even = position % 2 == 0
    copies = []
    for side, start in enumerate((0, rows - 8)):
        window = pl.ds(start, 8)
        for n, (src, dst) in enumerate(((image, img_e), (gx, gx_e))):
            copies.append(pltpu.make_async_copy(src.at[:, window, :], dst.at[side], sem.at[side, n]))
        copies.append(pltpu.make_async_copy(classes.at[window, :], cls_e.at[side], sem.at[side, 2]))
    for copy in copies:
        copy.start()
    low_half = sublane_ids() < 4
    ones = jnp.ones((8, rows), bf16)
    for k in range(channels):
        total = jnp.zeros((8, LANES), f32)
        for at in range(0, width, 512):
            part = jnp.dot(ones, gy[k, :, at : at + 512], preferred_element_type=f32)
            for i in range(0, 512, LANES):
                total = total + part[:, i : i + LANES]
        total = jnp.sum(total[:1], axis=1, keepdims=True) / width
        sums[k : k + 1, :] = jnp.broadcast_to(total, (1, LANES))
    for copy in copies:
        copy.wait()
    for k in range(channels):
        lead = jnp.zeros((8, LANES), f32)
        for j in range(tiles):
            lead = lead + img_e[0, k, :, lane_tile(j)]
        lead = jnp.sum(lead[0:1, :], axis=1, keepdims=True) / width
        lead = jnp.where(position == 0, lead, 0.0)
        sums[channels + k : channels + k + 1, :] = jnp.broadcast_to(lead, (1, LANES))
    if 2 * channels < 8:
        sums[2 * channels :, :] = jnp.zeros((8 - 2 * channels, LANES), f32)

    def joined(side, first, second):
        if side == 0:
            return jnp.where(low_half, first, pltpu.roll(second, 4, 0))
        return jnp.where(low_half, pltpu.roll(first, 4, 0), second)

    def fill(side, out):
        def one(j):
            at = pl.ds(pl.multiple_of(j * LANES, LANES), LANES)
            for k in range(channels):
                x = img_e[side, k, :, at]
                high = x.astype(bf16).astype(f32)
                out[2 * k, :, at] = joined(side, high, x - high).astype(bf16)
                y = gy[k, pl.ds(side * (rows - 8), 8), at].astype(f32)
                out[2 * k + 1, :, at] = joined(side, gx_e[side, k, :, at].astype(f32), y).astype(bf16)
            c = cls_e[side, :, at].astype(f32)
            out[2 * channels, :, at] = joined(side, c, c).astype(bf16)

        def step(j, carry):
            one(j)
            return carry

        lax.fori_loop(0, tiles, step, 0, unroll=8)

    @pl.when(even)
    def _():
        fill(1, to_a)
        fill(0, to_b)

    @pl.when(jnp.logical_not(even))
    def _():
        fill(0, to_a)
        fill(1, to_b)


def pack(image, gx, gy, classes):
    channels, rows, width = image.shape
    hbm = pl.BlockSpec(memory_space=pl.ANY)
    vmem = pl.BlockSpec(memory_space=pltpu.VMEM)
    edge = pltpu.VMEM((2 * channels + 1, 8, width), bf16)
    return pl.pallas_call(
        pack_kernel,
        out_shape=(edge, edge, pltpu.VMEM((8, LANES), f32)),
        in_specs=[hbm, hbm, hbm, vmem],
        out_specs=[vmem] * 3,
        scratch_shapes=[
            pltpu.VMEM((2, channels, 8, width), f32),
            pltpu.VMEM((2, channels, 8, width), bf16),
            pltpu.VMEM((2, 8, width), jnp.int32),
            pltpu.SemaphoreType.DMA((2, 3)),
        ],
        compiler_params=pltpu.CompilerParams(vmem_limit_bytes=SCOPED),
        name="pack",
    )(image, gx, classes, gy)


def factors(c, cover):
    w = cover * SCREEN * jnp.exp2(c)
    q = OMEGA / (w + 6.0)
    return q, q * w


def mend_column_seams(x_s, at, half, own_right, per_tile, tiles):
    lanes = lane_ids()
    count = 4 if half else 8
    for b in range(tiles // per_tile - 1):
        j = (b + 1) * per_tile - 1
        left = x_s[j, pl.ds(at, 8), :]
        right = x_s[j + 1, pl.ds(at, 8), :]
        in_right = jnp.where(lanes < BAND, right, 0.0)
        in_left = jnp.where((lanes >= LANES - 1 - BAND) & (lanes < LANES - 1), left, 0.0)
        band = jnp.where(own_right[b], in_right, in_left)
        mean = jnp.sum(band, axis=1, keepdims=True) / BAND
        x_s[j, pl.ds(at, count), :] = jnp.where(lanes == LANES - 1, mean, left)[:count]


def constant_terms(at, x_s, y_s, s_s, q_s, qw_of, b_s, tiles):
    lanes = lane_ids()
    first_lane, last_lane = lanes == 0, lanes == LANES - 1
    zero = jnp.zeros((8, LANES), f32)

    def load(j):
        x = x_s[j, pl.ds(at, 8), :]
        xu = x_s[j, pl.ds(at - 1, 8), :]
        y = y_s[j, pl.ds(at, 8), :]
        yu = y_s[j, pl.ds(at - 1, 8), :]
        f = 3.0 * x + xu
        base = f + 2.0 * (y - 2.0 * yu)
        return base, pltpu.roll(y - f, 1, 1), pltpu.roll(y, LANES - 1, 1)

    prev_rot = zero
    cur = load(0)
    for j in range(tiles):
        nxt = load(j + 1) if j + 1 < tiles else (None, None, zero)
        base, rot_l, rot_r = cur
        twice = base + jnp.where(first_lane, prev_rot, rot_l) + jnp.where(last_lane, nxt[2], rot_r)
        q = q_s[j, pl.ds(at, 8), :]
        b_s[j, pl.ds(at, 8), :] = qw_of(j, q) * s_s[j, pl.ds(at, 8), :] - (0.5 * q) * twice
        prev_rot = rot_l
        cur = nxt


def weight_part(j, q):
    return OMEGA - 6.0 * q


def prepare_kernel(validity, owners, image, gx, gy, classes, s_o, b_o, x_o, y_o, q_s, row_y, row_i, level):
    channels, rows, width = image.shape
    tiles = width // LANES
    per_tile = TILE_COLS // LANES
    position = lax.axis_index("row")
    tile_row = position * rows // TILE_ROWS
    covers = [validity[tile_row, b].astype(f32) for b in range(width // TILE_COLS)]
    own_right = [owners[tile_row, 1, b] == 1 for b in range(width // TILE_COLS - 1)]

    def weights(g, carry):
        at = pl.multiple_of(g * 8, 8)
        for j in range(tiles):
            q, _ = factors(classes[pl.ds(at, 8), lane_tile(j)].astype(f32), covers[j // per_tile])
            q_s[j, pl.ds(FIRST + at, 8), :] = q
        return carry

    lax.fori_loop(0, rows // 8, weights, 0)

    r = lax.broadcasted_iota(jnp.int32, (rows, rows), 0)
    c = lax.broadcasted_iota(jnp.int32, (rows, rows), 1)
    above = jnp.where(c < r, 1.0, 0.0)

    def channel(k, carry):
        s_s, b_s, x_s, y_s = s_o.at[k], b_o.at[k], x_o.at[k], y_o.at[k]

        def unpack(g, carry):
            at = pl.multiple_of(g * 16, 16)
            sum_y = jnp.zeros((16, LANES), f32)
            sum_i = jnp.zeros((16, LANES), f32)
            for j in range(tiles):
                here = pl.ds(FIRST + at, 16)
                x_s[j, here, :] = gx[k, pl.ds(at, 16), lane_tile(j)].astype(f32)
                y = gy[k, pl.ds(at, 16), lane_tile(j)].astype(f32)
                y_s[j, here, :] = y
                sum_y = sum_y + y
                sum_i = sum_i + image[k, pl.ds(at, 16), lane_tile(j)]
            row_y[pl.ds(at, 16), :] = sum_y
            row_i[pl.ds(at, 16), :] = sum_i
            return carry

        lax.fori_loop(0, rows // 16, unpack, 0)
        climbed = jnp.dot(above, row_y[...], precision=lax.Precision.HIGHEST, preferred_element_type=f32)
        lv = jnp.sum(climbed - row_i[...], axis=1, keepdims=True) / width
        level[...] = jnp.broadcast_to(lv, (rows, LANES))
        for g in range(rows // 8):
            mend_column_seams(x_s, FIRST + 8 * g, False, own_right, per_tile, tiles)
            lv = level[8 * g : 8 * g + 8, :]
            for j in range(tiles):
                s_s[j, FIRST + 8 * g : FIRST + 8 * g + 8, :] = image[k, 8 * g : 8 * g + 8, lane_tile(j)] + lv
        for g in range((rows + 2 * HALO) // 8 - 2):
            constant_terms(TOP + 8 + 8 * g, x_s, y_s, s_s, q_s, weight_part, b_s, tiles)
        return carry

    lax.fori_loop(0, channels, channel, 0)


def prepare(validity, owners, image, gx, gy, classes):
    channels, rows, width = image.shape
    tiles = width // LANES
    tall = TOP + rows + 2 * HALO + 8
    smem = pl.BlockSpec(memory_space=pltpu.SMEM)
    vmem = pl.BlockSpec(memory_space=pltpu.VMEM)
    big = pltpu.VMEM((channels, tiles, tall, LANES), f32)
    return pl.pallas_call(
        prepare_kernel,
        out_shape=(big, big, big, big, pltpu.VMEM((tiles, tall, LANES), f32)),
        in_specs=[smem, smem, vmem, vmem, vmem, vmem],
        out_specs=[vmem] * 5,
        scratch_shapes=[pltpu.VMEM((rows, LANES), f32)] * 3,
        compiler_params=pltpu.CompilerParams(vmem_limit_bytes=SCOPED),
        name="prepare",
    )(validity, owners, image, gx, gy, classes)


def sweep_kernel(
    validity, owners, offset, sums, from_a, from_b, s_i, b_i, x_i, y_i, q_i,
    out, s_o, b_o, x_o, y_o, q_s, t_s, stage, sem,
):
    channels, tiles, tall, _ = s_o.shape
    rows = tall - 2 * HALO - TOP - 8
    groups = (rows + 2 * HALO) // 8
    per_tile = TILE_COLS // LANES
    position = lax.axis_index("row")
    last = lax.axis_size("row") - 1
    even = position % 2 == 0
    there = (position > 0, position < last)
    beyond = (
        jnp.maximum(position * rows - 1, 0) // TILE_ROWS,
        jnp.minimum((position + 1) * rows, (last + 1) * rows - 1) // TILE_ROWS,
    )
    own_right = [[owners[t, 1, b] == 1 for b in range(tiles // per_tile - 1)] for t in beyond]
    lanes = lane_ids()
    first_lane, last_lane = lanes == 0, lanes == LANES - 1
    upper = sublane_ids() < HALO

    def halo_of(side, n, j):
        one, other = (from_b, from_a) if side == 0 else (from_a, from_b)
        return jnp.where(even, one[n, :, lane_tile(j)], other[n, :, lane_tile(j)])

    ends = (TOP, FIRST + rows)
    for side, at in enumerate(ends):
        for j in range(tiles):
            cover = validity[beyond[side], j // per_tile].astype(f32)
            q, _ = factors(halo_of(side, 2 * channels, j).astype(f32), cover)
            q_s[j, at : at + HALO, :] = jnp.where(there[side], q, 0.0)[:HALO]

    def channel(k, carry):
        s_s, b_s, x_s, y_s = s_o.at[k], b_o.at[k], x_o.at[k], y_o.at[k]
        c = jnp.broadcast_to(offset[pl.ds(k, 1), :] + offset[pl.ds(k + channels, 1), :], (8, LANES))
        total = jnp.broadcast_to(sums[pl.ds(k, 1), :], (8, LANES))

        for side, at in enumerate(ends):
            sum_y = jnp.zeros((8, LANES), f32)
            sum_i = jnp.zeros((8, LANES), f32)
            for j in range(tiles):
                v = halo_of(side, 2 * k, j).astype(f32)
                i = v + pltpu.roll(v, 4, 0)
                s_s[j, at : at + HALO, :] = i[:HALO]
                g = halo_of(side, 2 * k + 1, j).astype(f32)
                y = pltpu.roll(g, 4, 0)
                x_s[j, at : at + HALO, :] = g[:HALO]
                y_s[j, at : at + HALO, :] = y[:HALO]
                sum_y = sum_y + y
                sum_i = sum_i + i
            mean_y = jnp.where(upper, jnp.sum(sum_y, axis=1, keepdims=True) / (tiles * LANES), 0.0)
            mean_i = jnp.sum(sum_i, axis=1, keepdims=True) / (tiles * LANES)
            if side == 0:
                fall = mean_y + pltpu.roll(mean_y, 7, 0)
                lv = -(fall + pltpu.roll(fall, 6, 0)) - mean_i
            else:
                climb = pltpu.roll(mean_y, 1, 0)
                climb = climb + pltpu.roll(climb, 1, 0)
                lv = total + (climb + pltpu.roll(climb, 2, 0)) - mean_i
            for j in range(tiles):
                v = s_s[j, pl.ds(at, 8), :] + lv
                s_s[j, at : at + HALO, :] = jnp.where(there[side], v, -c)[:HALO]
            mend_column_seams(x_s, at, True, own_right[side], per_tile, tiles)

        for side, at in ((0, TOP), (1, TOP + 8 * groups - 8)):
            constant_terms(at, x_s, y_s, s_s, q_s, weight_part, b_s, tiles)
            for j in range(tiles):
                v = b_s[j, ends[side] : ends[side] + HALO, :]
                b_s[j, ends[side] : ends[side] + HALO, :] = jnp.where(there[side], v, -OMEGA * c[:HALO])

        beyond_lane = -2.0 * c

        def sweep(src, at, write):
            def load(j):
                s = src[j, pl.ds(at, 8), :]
                u = src[j, pl.ds(at - 1, 8), :] + src[j, pl.ds(at + 1, 8), :]
                a = s + 0.5 * u
                return s, u, pltpu.roll(a, 1, 1), pltpu.roll(a, LANES - 1, 1)

            prev_rot = beyond_lane
            cur = load(0)
            for j in range(tiles):
                nxt = load(j + 1) if j + 1 < tiles else (None, None, None, beyond_lane)
                s, u, rot_l, rot_r = cur
                n = u + jnp.where(first_lane, prev_rot, rot_l) + jnp.where(last_lane, nxt[3], rot_r)
                write(j, (1.0 - OMEGA) * s + (q_s[j, pl.ds(at, 8), :] * n + b_s[j, pl.ds(at, 8), :]))
                prev_rot = rot_l
                cur = nxt

        src, dst = s_s, t_s
        for _ in range(SWEEPS - 1):
            for g in range(groups):
                at = TOP + 8 * g

                def keep(j, v, at=at, dst=dst):
                    dst[j, at : at + 8, :] = v

                sweep(src, at, keep)
            src, dst = dst, src
        for g in range(rows // 8):

            def finish(j, v, g=g):
                stage[k, 8 * g : 8 * g + 8, lane_tile(j)] = v + c

            sweep(src, FIRST + 8 * g, finish)
        pltpu.make_async_copy(stage.at[k], out.at[k], sem.at[k]).start()
        return carry

    lax.fori_loop(0, channels, channel, 0)
    for k in range(channels):
        pltpu.make_async_copy(stage.at[k], out.at[k], sem.at[k]).wait()


def sweeps(validity, owners, offset, sums, from_a, from_b, parts, out_shape):
    channels, tiles, tall, _ = parts[0].shape
    smem = pl.BlockSpec(memory_space=pltpu.SMEM)
    vmem = pl.BlockSpec(memory_space=pltpu.VMEM)
    parts = [pltpu.with_memory_space_constraint(p, pltpu.VMEM) for p in parts]
    return pl.pallas_call(
        sweep_kernel,
        out_shape=[jax.ShapeDtypeStruct(out_shape, f32)] + [pltpu.VMEM(p.shape, f32) for p in parts],
        in_specs=[smem, smem] + [vmem] * (4 + len(parts)),
        out_specs=[pl.BlockSpec(memory_space=pl.ANY)] + [vmem] * len(parts),
        input_output_aliases={6 + n: 1 + n for n in range(len(parts))},
        scratch_shapes=[
            pltpu.VMEM((tiles, tall, LANES), f32),
            pltpu.VMEM(out_shape, f32),
            pltpu.SemaphoreType.DMA((channels,)),
        ],
        compiler_params=pltpu.CompilerParams(vmem_limit_bytes=SCOPED),
        name="sweeps",
    )(validity, owners, offset, sums, from_a, from_b, *parts)[0]


def pairs_with(offset, devices):
    pairs = []
    for i in range(offset, devices - 1, 2):
        pairs += [(i, i + 1), (i + 1, i)]
    return pairs


def carried_in(sums, channels):
    devices = lax.axis_size("row")
    position = lax.axis_index("row")
    is_total = lax.broadcasted_iota(jnp.int32, sums.shape, 0) < channels
    held, carried = sums, jnp.where(is_total, 0.0, sums)
    by = 1
    while by < devices:
        pairs = [(i, i ^ by) for i in range(devices) if (i ^ by) < devices]
        other = lax.ppermute(held, "row", pairs)
        lower = (position & by) != 0
        carried = carried + jnp.where(is_total & jnp.logical_not(lower), 0.0, other)
        held = held + other
        by *= 2
    return carried


def blended_last_row(gy, owners):
    rows, width = gy.shape[1:]
    devices, position = lax.axis_size("row"), lax.axis_index("row")
    vertical = gy.astype(f32)
    own = lax.dynamic_index_in_dim(owners, position * rows // TILE_ROWS, 0, keepdims=False)
    pairs = [(i, i - 1) for i in range(1, devices)]
    lower = lax.ppermute(jnp.mean(vertical[:, :BAND], axis=1).astype(bf16), "row", pairs)
    upper = jnp.mean(vertical[:, rows - 1 - BAND : rows - 1], axis=1).astype(bf16)
    lower_owns = jnp.repeat(own[:, 0], TILE_COLS, total_repeat_length=width)[None] == 1
    at_seam = (((position + 1) * rows) % TILE_ROWS == 0) & (position < devices - 1)
    last = jnp.where(at_seam, jnp.where(lower_owns, lower, upper), gy[:, -1])
    return gy.at[:, -1].set(last)


def per_device(image, grad_x, grad_y, classes, validity, owners):
    channels, rows, _ = image.shape
    devices = lax.axis_size("row")
    if devices * rows > TILE_ROWS:
        grad_y = blended_last_row(grad_y, owners)
    owners = jnp.transpose(owners, (0, 2, 1))
    to_a, to_b, sums = pack(image, grad_x, grad_y, classes)
    from_a = lax.ppermute(to_a, "row", pairs_with(0, devices))
    from_b = lax.ppermute(to_b, "row", pairs_with(1, devices))
    offset = carried_in(sums, channels)
    parts = prepare(validity, owners, image, grad_x, grad_y, classes)
    return sweeps(validity, owners, offset, sums, from_a, from_b, parts, image.shape)


def solution(mesh):
    split = ("win", "row")
    in_specs = (
        P(None, split, None), P(None, split, None), P(None, split, None),
        P(split, None), P("win", None), P("win", None, None),
    )
    return jax.shard_map(
        per_device, mesh=mesh, in_specs=in_specs, out_specs=P(None, split, None), check_vma=False
    )
```
